256 devices in a mesh: dp: 32 (over x_lo, z, core), tensor: 8 (over x_hi, y).
Axes of the slice: x: 4 (x_hi: 2, x_lo: 2; x = x_hi * 2 + x_lo), y: 4, z: 8, core: 2. Of those that a mesh axis runs over, the one named last changes fastest.
Arguments:
- drafter_hidden: bfloat16 [2, 4096, 4096], P(None, 'dp', 'tensor'), may hold values from -2000 to 2000
- norm_gain: bfloat16 [4096], P('tensor'), may hold values from 0.5 to 1.5
- head_weight: bfloat16 [4096, 16384], P('tensor', 'dp'), may hold values from -24 to 24
- labels: int32 [4096], P('dp'), may hold values from 0 to 16383
- loss_mask: int32 [4096], P('dp'), may hold values 0 or 1
- offsets: int32 [2], replicated, may hold values from 1 to 4
Outputs:
- draft_loss: float32 [], replicated
- head_grad: float32 [4096, 16384], P('tensor', 'dp')
The draws below stay inside these ranges and needn't reach their ends.
All inputs are finite; a program needn't handle non-finite values. No bound on the sum of `loss_mask` on one device may be relied on, other than what follows from the above.
Results may differ from the reference program's by a relative error of at most 0.0048.
Values may be sent and summed in bfloat16 or wider, within the bound.
No kernel may reach another device: no remote copies, remote signals or barrier semaphores. Data moves between devices by JAX's collectives and lax.ppermute only.
A program may use at most 128 MiB of HBM per device.

```python
import math
import jax
import jax.numpy as jnp
from jax import lax

D = 4096
STEPS = 2
WINDOW = 512
MAXOFF = 4
TOKENS = 4096
VOCAB = 16384


def shared_head(key):
    head_key = jax.random.fold_in(key, 11)
    values = jax.random.truncated_normal(head_key, -6.0, 6.0, (D, VOCAB), jnp.float32)
    loud = max(1.0, 48.0 / math.sqrt(D))
    column_ids = jnp.arange(VOCAB)
    boost = jnp.where(column_ids % 8 == 3, loud, 1.0).astype(jnp.float32)
    return values * (5.0 / math.sqrt(D)) * boost[None, :]


def draw_head_weight(key, part):
    return shared_head(key).astype(jnp.bfloat16)


def draw_drafter_hidden(key, part):
    noise_key = jax.random.fold_in(key, 21)
    scale_key = jax.random.fold_in(key, 22)
    first_key = jax.random.fold_in(key, 24)
    second_key = jax.random.fold_in(key, 25)
    noise = jax.random.truncated_normal(noise_key, -6.0, 6.0, (STEPS, TOKENS, D), jnp.float32)
    row_scale = jnp.exp(jax.random.uniform(scale_key, (STEPS, TOKENS, 1), jnp.float32, 0.0, math.log(10.0)))
    head_rows = shared_head(key).T
    groups = VOCAB // 8
    first = 8 * jax.random.randint(first_key, (STEPS, TOKENS), 0, groups) + 3
    second = (first + 8 * jax.random.randint(second_key, (STEPS, TOKENS), 1, groups)) % VOCAB
    positions = jnp.arange(TOKENS)
    chosen = (positions % 61 == 7)[None, :, None]
    strengths = jnp.array([0.5, 1.0, 2.0, 3.0], jnp.float32)[positions // 61 % 4][None, :, None]
    signal = strengths * 8.0 * (head_rows[first] + 0.99 * head_rows[second])
    mixed = jnp.where(chosen, noise + signal, noise)
    return jnp.clip(mixed * row_scale, -2000.0, 2000.0).astype(jnp.bfloat16)


def with_ends(drawn, stream_key, least, top_value):
    place = [jax.random.randint(jax.random.fold_in(stream_key, axis), (), 0, length) for axis, length in enumerate(drawn.shape)]
    widest = drawn.shape.index(max(drawn.shape))
    beside = place[:widest] + [(place[widest] + 1) % drawn.shape[widest]] + place[widest + 1:]
    return drawn.at[tuple(place)].set(least).at[tuple(beside)].set(top_value)


def setup_inputs(seed: int = 0) -> dict:
    streams_of = jax.random.split(jax.random.key(seed), 7)
    drafter_hidden = draw_drafter_hidden(jax.random.fold_in(streams_of[6], 71), 0)
    norm_gain = jnp.clip(1.0 + 0.1 * jax.random.normal(streams_of[1], (D,), jnp.float32), 0.5, 1.5).astype(jnp.bfloat16)
    head_weight = draw_head_weight(jax.random.fold_in(streams_of[6], 71), 0)
    labels = with_ends(jax.random.randint(streams_of[3], (TOKENS,), 0, VOCAB), jax.random.fold_in(streams_of[3], 1), 0, VOCAB - 1).astype(jnp.int32)
    loss_mask = with_ends((jax.random.randint(streams_of[4], (TOKENS,), 0, 4) < 3).astype(jnp.int32), jax.random.fold_in(streams_of[4], 1), 0, 1)
    offsets = jax.random.randint(streams_of[5], (STEPS,), 1, MAXOFF + 1).astype(jnp.int32)
    return dict(drafter_hidden=drafter_hidden, norm_gain=norm_gain, head_weight=head_weight, labels=labels, loss_mask=loss_mask, offsets=offsets)


epsilon = 1e-05
step_decay = 0.8

def reference(drafter_hidden, norm_gain, head_weight, labels, loss_mask, offsets):
    hidden_wide = drafter_hidden.astype(jnp.float32)
    inverse = lax.rsqrt(lax.optimization_barrier(jnp.mean(hidden_wide * hidden_wide, axis=-1, keepdims=True)) + epsilon)
    normed = (hidden_wide * inverse * norm_gain.astype(jnp.float32)).astype(jnp.bfloat16)
    weight_wide = head_weight.astype(jnp.float32)
    positions = jnp.arange(TOKENS, dtype=jnp.int32)
    columns = jnp.arange(VOCAB, dtype=jnp.int32)
    block_rows = min(512, TOKENS)
    gradient = jnp.zeros((D, VOCAB), jnp.float32)
    loss_total = jnp.zeros((), jnp.float32)
    for step_at in range(STEPS):
        factor = step_decay ** step_at
        inside = positions % WINDOW + offsets[step_at] < WINDOW
        clamped = jnp.minimum(positions + offsets[step_at], TOKENS - 1).astype(jnp.int32)
        row_label = labels[clamped]
        row_weight = jnp.where(inside, loss_mask[clamped], 0).astype(jnp.float32)
        counted = jnp.sum(row_weight)
        rows_step = normed[step_at]

        def one_block(state_pair, number):
            offset_row = (number * block_rows).astype(jnp.int32)
            row_block = lax.dynamic_slice_in_dim(rows_step, offset_row, block_rows, 0)
            block_label = lax.dynamic_slice_in_dim(row_label, offset_row, block_rows, 0)
            block_weight = lax.dynamic_slice_in_dim(row_weight, offset_row, block_rows, 0)
            rows_wide = row_block.astype(jnp.float32)
            logits = jnp.dot(rows_wide, weight_wide, precision=lax.Precision.HIGHEST)
            row_top = lax.optimization_barrier(jnp.max(logits, axis=-1))
            total_exp = lax.optimization_barrier(jnp.sum(jnp.exp(logits - row_top[:, None]), axis=-1))
            log_total = row_top + jnp.log(total_exp)
            hitting = columns[None, :] == block_label[:, None]
            label_logit = lax.optimization_barrier(jnp.sum(jnp.where(hitting, logits, 0.0), axis=-1))
            numerator = jnp.sum(block_weight * (log_total - label_logit))
            softmax = jnp.exp(logits - log_total[:, None])
            slopes = (factor * block_weight[:, None] * (softmax - hitting.astype(jnp.float32))).astype(jnp.bfloat16)
            update = jnp.dot(rows_wide.T, slopes.astype(jnp.float32), precision=lax.Precision.HIGHEST)
            return ((state_pair[0] + update, state_pair[1] + numerator), None)
        start_pair = (gradient, jnp.zeros((), jnp.float32))
        finished, ignored = lax.scan(one_block, start_pair, jnp.arange(TOKENS // block_rows, dtype=jnp.int32))
        gradient = finished[0]
        loss_total = loss_total + factor * finished[1] / counted
    return (loss_total, gradient)
```

```python
import jax
import jax.numpy as jnp
import numpy as np
from jax import lax
from jax.sharding import Mesh
from jax.sharding import PartitionSpec as P

WINDOW = 512
LOOKAHEAD = 4
META = 128

epsilon = 1e-05
step_decay = 0.8

f32 = jnp.float32
bf16 = jnp.bfloat16


def along_x(value, by):
    place = lambda p: (p % 2) * 2 + p // 2
    return lax.ppermute(value, ("xl", "xh"), [(place(p), place((p + by) % 4)) for p in range(4)])


def along(value, axis, by):
    n = lax.axis_size(axis)
    return lax.ppermute(value, axis, [(i, (i + by) % n) for i in range(n)])


def other_core(value):
    return lax.ppermute(value, "c", [(0, 1), (1, 0)])


def crossed(value):
    swapped = lax.ppermute(value, ("c", "xh"), [(1, 2), (2, 1)])
    stays = lax.axis_index("c") == lax.axis_index("xh")
    return jnp.where(stays, value, swapped)


def block_order():
    near, distant = (0, 7, 1), (6, 2, 5, 3, 4)
    xs = (0, 3, 1, 2)
    first = lambda hops, zs: [(0, a, b) for a in hops for b in zs]
    second = lambda zs: [(1, a, b) for b in zs for a in xs]
    return (
        first((0,), near) + first((0,), distant) + second((0, 7, 1))
        + first(xs[1:], near) + second((6, 2))
        + first(xs[1:], distant) + second((5, 3, 4))
    )


def sent_to_all(value, axis):
    copies = jnp.broadcast_to(value, (lax.axis_size(axis), *value.shape))
    return lax.all_to_all(copies, axis, split_axis=0, concat_axis=0, tiled=True)


def ring_of_four(piece, move):
    half = piece.shape[0] // 2
    ahead, behind = move(piece, 1), move(piece, -1)
    far = [move(ahead[:half], 1), move(behind[half:], -1)]
    return ahead, behind, far


def row_facts(labels, loss_mask, offsets, steps):
    local_tokens = labels.shape[0]
    ways = lax.axis_size(("xl", "z", "c"))
    rank = lax.axis_index(("xl", "z", "c"))
    slab = local_tokens // 8
    both = jnp.stack([labels, loss_mask])
    following = lax.ppermute(both, ("xl", "z", "c"), [(i, (i - 1) % ways) for i in range(ways)])
    following = jnp.where(rank == ways - 1, both[:, -1:], following)
    longer = jnp.concatenate([both, following], axis=1)
    at = lax.axis_index(("xh", "y")) * slab
    found = []
    for step in range(steps):
        piece = lax.dynamic_slice(longer, (0, at + offsets[step]), (2, slab))
        position = rank * local_tokens + at + jnp.arange(slab, dtype=jnp.int32)
        inside = position % WINDOW + offsets[step] < WINDOW
        found.append(
            jnp.stack([piece[0] // 128, piece[0] % 128, jnp.where(inside, piece[1], 0)], axis=-1)
        )
    facts = jnp.stack(found).astype(bf16)
    return jnp.pad(facts, ((0, 0), (0, 0), (0, META - facts.shape[-1])))


def local(drafter_hidden, norm_gain, head_weight, labels, loss_mask, offsets):
    steps, local_tokens, width_part = drafter_hidden.shape
    vocab_part = head_weight.shape[1]
    width = width_part * 8
    slab = local_tokens // 8
    core, half_x, row_y = lax.axis_index("c"), lax.axis_index("xh"), lax.axis_index("y")

    with jax.named_scope("head_gather"):
        piece = crossed(head_weight)
        ahead, behind, far = ring_of_four(piece, lambda v, by: along(v, "y", by))
        half = jnp.zeros((4, width_part, vocab_part), bf16)
        for back, part in ((0, piece), (1, ahead), (3, behind), (2, jnp.concatenate(far))):
            half = lax.dynamic_update_slice(half, part[None], ((row_y - back) % 4, 0, 0))
        head = jnp.zeros((2, 4, width_part, vocab_part), bf16)
        head = lax.dynamic_update_slice(head, half[None], (core, 0, 0, 0))
        head = lax.dynamic_update_slice(head, other_core(half)[None], (1 - core, 0, 0, 0))
        head = head.reshape(width, vocab_part)

    with jax.named_scope("normed_rows"):
        facts = row_facts(labels, loss_mask, offsets, steps)
        parts = drafter_hidden.reshape(steps, 8, slab, width_part).swapaxes(0, 1)
        parts = parts.reshape(8, steps * slab, width_part)
        gains = jnp.broadcast_to(norm_gain, (8, 8, width_part))
        traded = lax.all_to_all(
            jnp.concatenate([parts, gains], axis=1), ("xh", "y"), split_axis=0, concat_axis=0, tiled=True
        )
        gain = traded[:, steps * slab].reshape(width)
        hidden = traded[:, : steps * slab].swapaxes(0, 1).reshape(steps * slab, width).astype(f32)
        inverse = lax.rsqrt(jnp.mean(hidden * hidden, axis=-1, keepdims=True) + epsilon)
        normed = (hidden * inverse * gain.astype(f32)).astype(bf16)
        rows = jnp.concatenate([normed, facts.reshape(steps * slab, META)], axis=1)

    with jax.named_scope("rows_gather"):
        first, second = rows[:slab], rows[slab:]
        up = lambda v: along(v, "z", 1)
        down = lambda v: along(v, "z", -1)
        u1, d1 = up(first), down(first)
        near = jnp.concatenate([first, u1, d1])
        near_x = ring_of_four(near, along_x)
        u2, d2 = up(u1), down(d1)
        u3, d3 = up(u2), down(d2)
        u4 = up(u3)
        distant = jnp.concatenate([u2, d2, u3, d3, u4])
        distant_x = ring_of_four(distant, along_x)
        ahead, behind, far = ring_of_four(second, along_x)
        own = jnp.concatenate([second, ahead, behind, *far])
        v1, e1 = up(own), down(own)
        v2, e2 = up(v1), down(e1)
        v3, e3 = up(v2), down(e2)
        part = own.shape[0] // 2
        v4, e4 = up(v3[:part]), down(e3[part:])

    flat = lambda group: [group[0], group[1], *group[2]]
    groups = [
        ([near, distant], [own, v1, e1]),
        (flat(near_x), [v2, e2]),
        (flat(distant_x), [v3, e3, v4, e4]),
    ]
    xs, ls, fs, ks = [], [], [], []
    with jax.named_scope("logits"):
        for early, late in groups:
            x = jnp.concatenate(early + late)
            count = sum(p.shape[0] for p in early)
            xs.append(x)
            fs.append(x[:, width : width + 3].astype(f32))
            ks.append(jnp.arange(x.shape[0]) >= count)
            ls.append(jnp.dot(x[:, :width], head, preferred_element_type=f32))
        facts = jnp.concatenate(fs)
        is_second = jnp.concatenate(ks)
        row_label = (facts[:, 0] * 128 + facts[:, 1]).astype(jnp.int32)
        row_weight = facts[:, 2]
        block = lax.axis_index(("xl", "z", "xh"))
        columns = block * vocab_part + jnp.arange(vocab_part, dtype=jnp.int32)
        logits = jnp.concatenate(ls)
        hitting = columns[None, :] == row_label[:, None]
        top = jnp.max(logits, axis=-1)
        part_lse = top + jnp.log(jnp.sum(jnp.exp(logits - top[:, None]), axis=-1))
        part_label = jnp.sum(jnp.where(hitting, logits, 0.0), axis=-1)

    with jax.named_scope("row_totals"):
        order = np.array(block_order(), np.int32)
        place = np.zeros((2, 4, 8), np.int32)
        place[tuple(order.T)] = np.arange(len(order))
        x_at, z_at = 2 * half_x + lax.axis_index("xl"), lax.axis_index("z")
        slot = order[:, 0] * 32 + (order[:, 1] + x_at) % 4 * 8 + (order[:, 2] + z_at) % 8
        turned = jnp.roll(jnp.asarray(place), (x_at, z_at), (1, 2)).reshape(-1)
        pair = jnp.concatenate([part_lse.reshape(64, -1)[turned], part_label.reshape(64, -1)[turned]])
        stats = sent_to_all(pair, ("xl", "z", "xh"))
        each, picked = stats[:, :64], stats[:, 64:]
        peak = jnp.max(each, axis=0)
        lse = peak + jnp.log(jnp.sum(jnp.exp(each - peak), axis=0))
        cross = (lse - jnp.sum(picked, axis=0))[slot].reshape(-1)
        lse = lse[slot].reshape(-1)

    with jax.named_scope("gradient"):
        factor = jnp.where(is_second, step_decay, 1.0).astype(f32)
        softmax = jnp.exp(logits - lse[:, None])
        slopes = ((factor * row_weight)[:, None] * (softmax - hitting.astype(f32))).astype(bf16)
        x = jnp.concatenate(xs)[:, :width].reshape(-1, 2, 4 * width_part)
        mine = lax.dynamic_index_in_dim(x, core, 1, keepdims=False)
        theirs = lax.dynamic_index_in_dim(x, 1 - core, 1, keepdims=False)
        outer = lambda a: jnp.einsum("rd,rv->dv", a, slopes, preferred_element_type=f32)
        to_core = other_core(outer(theirs).astype(bf16))
        both = (outer(mine) + to_core.astype(f32)).reshape(4, width_part, vocab_part)
        total = lax.dynamic_index_in_dim(both, row_y, 0, keepdims=False)
        for by in (2, 1, 3):
            block = lax.dynamic_index_in_dim(both, (row_y + by) % 4, 0, keepdims=False)
            total = total + along(block.astype(bf16), "y", by).astype(f32)
        grad = jnp.where(
            core == half_x,
            total,
            lax.ppermute(total.astype(bf16), ("c", "xh"), [(1, 2), (2, 1)]).astype(f32),
        )

    with jax.named_scope("loss"):
        sums = jnp.stack(
            [
                jnp.sum(jnp.where(is_second == (k == 1), v, 0.0))
                for v in (row_weight * cross, row_weight)
                for k in range(steps)
            ]
        )
        sums = sent_to_all(sums[None], ("c", "y")).sum(axis=(0, 1))
        factors = step_decay ** jnp.arange(steps, dtype=f32)
        loss = jnp.sum(factors * sums[:steps] / sums[steps:])
    return loss, grad


def solution(mesh):
    inner = Mesh(mesh.devices.reshape(2, 8, 2, 2, 4), ("xl", "z", "c", "xh", "y"))
    dp, tensor = ("xl", "z", "c"), ("xh", "y")
    return jax.shard_map(
        local,
        mesh=inner,
        in_specs=(P(None, dp, tensor), P(tensor), P(tensor, dp), P(dp), P(dp), P()),
        out_specs=(P(), P(tensor, dp)),
        check_vma=False,
    )
```

```python
import functools

import jax
import jax.numpy as jnp
import numpy as np
from jax import lax
from jax.experimental import pallas as pl
from jax.experimental.pallas import tpu as pltpu
from jax.sharding import Mesh
from jax.sharding import PartitionSpec as P

WINDOW = 512
META = 128
SLAB = 16

epsilon = 1e-05
step_decay = 0.8

f32 = jnp.float32
bf16 = jnp.bfloat16


def across_x(value, bits):
    place = lambda p: (p % 2) * 2 + p // 2
    return lax.ppermute(value, ("xl", "xh"), [(place(p), place(p ^ bits)) for p in range(4)])


def along(value, axis, by):
    n = lax.axis_size(axis)
    return lax.ppermute(value, axis, [(i, (i + by) % n) for i in range(n)])


def other_core(value):
    return lax.ppermute(value, "c", [(0, 1), (1, 0)])


def crossed(value):
    return lax.ppermute(value, ("c", "xh"), [(1, 2), (2, 1)])


def sent_to_all(value, axis):
    copies = jnp.broadcast_to(value, (lax.axis_size(axis), *value.shape))
    return lax.all_to_all(copies, axis, split_axis=0, concat_axis=0, tiled=True)


def together(*values):
    return lax.optimization_barrier(values)


def row_facts(labels, loss_mask, offsets, steps):
    local_tokens = labels.shape[0]
    ways = lax.axis_size(("xl", "z", "c"))
    rank = lax.axis_index(("xl", "z", "c"))
    both = jnp.stack([labels, loss_mask])
    following = lax.ppermute(both, ("xl", "z", "c"), [(i, (i - 1) % ways) for i in range(ways)])
    following = jnp.where(rank == ways - 1, both[:, -1:], following)
    longer = jnp.concatenate([both, following], axis=1)
    at = lax.axis_index(("xh", "y")) * SLAB
    found = []
    for step in range(steps):
        piece = lax.dynamic_slice(longer, (0, at + offsets[step]), (2, SLAB))
        position = rank * local_tokens + at + jnp.arange(SLAB, dtype=jnp.int32)
        inside = position % WINDOW + offsets[step] < WINDOW
        weight = jnp.where(inside, piece[1], 0)
        flag = jnp.full_like(weight, step)
        found.append(jnp.stack([piece[0] // 128, piece[0] % 128, weight, flag], axis=-1))
    facts = jnp.stack(found).astype(bf16).reshape(steps * SLAB, 4)
    return jnp.pad(facts, ((0, 0), (0, META - facts.shape[-1])))


VMEM = pl.BlockSpec(memory_space=pltpu.VMEM)
SMEM = pl.BlockSpec(memory_space=pltpu.SMEM)


def block_of(refs, counts, at, width):
    columns = pl.ds(pl.multiple_of(at, width), width)
    return jnp.concatenate([r[pl.ds(0, count), columns] for r, count in zip(refs, counts)])


def logits_of(pieces, head_mine, head_other, features):
    n, counts = len(pieces), [count for _, count in pieces]
    arrays, rows = [p for p, _ in pieces], sum(counts)
    _, depth, columns = head_mine.shape
    meta_at = arrays[0].shape[1] - META

    def kernel(features_ref, *refs):
        head_mine_ref, head_other_ref, out_ref, facts_ref = refs[n:]
        facts_ref[...] = block_of(refs[:n], counts, meta_at, META)
        for k in range(8):
            x = block_of(refs[:n], counts, features_ref[k] * depth, depth)
            head = (head_mine_ref, head_other_ref)[k // 4][k % 4]
            found = jnp.dot(x, head, preferred_element_type=f32)
            if k == 0:
                out_ref[...] = found
            else:
                out_ref[...] += found

    return pl.pallas_call(
        kernel,
        out_shape=(
            jax.ShapeDtypeStruct((rows, columns), f32),
            jax.ShapeDtypeStruct((rows, META), bf16),
        ),
        in_specs=[SMEM] + [VMEM] * (n + 2),
        out_specs=(VMEM, VMEM),
        compiler_params=pltpu.CompilerParams(vmem_limit_bytes=32 << 20),
        cost_estimate=pl.CostEstimate(
            flops=2 * rows * 8 * depth * columns,
            bytes_accessed=2 * 8 * depth * (rows + columns),
            transcendentals=0,
        ),
    )(features, *arrays, head_mine, head_other)


def diagonal():
    return lax.broadcasted_iota(jnp.int32, (128, 128), 0) == lax.broadcasted_iota(
        jnp.int32, (128, 128), 1
    )


def hits(facts, columns, first):
    label = (facts[:, 0:1] * 128.0 + facts[:, 1:2]).astype(jnp.int32) - first
    return lax.broadcasted_iota(jnp.int32, (facts.shape[0], columns), 1) == label


def chunks(groups):
    start = 0
    for g, group in enumerate(groups):
        rows = group.shape[0]
        size = max(k for k in range(SLAB, 81, SLAB) if rows % k == 0)
        for at in range(0, rows, size):
            yield g, at, start + at, size
        start += rows


def row_parts(scalars, logits, facts):
    n = len(logits)
    rows, columns = sum(v.shape[0] for v in logits), logits[0].shape[1]

    def kernel(scalars_ref, *refs):
        logit_refs, fact_refs, (out_ref, held) = refs[:n], refs[n : 2 * n], refs[2 * n :]
        for g, at, row, size in chunks(logits):
            values = logit_refs[g][pl.ds(at, size), :]
            fact = fact_refs[g][pl.ds(at, size), :].astype(f32)
            hit = hits(fact, columns, scalars_ref[128])
            top = jnp.max(values, axis=-1, keepdims=True)
            lse = top + jnp.log(jnp.sum(jnp.exp(values - top), axis=-1, keepdims=True))
            picked = jnp.sum(jnp.where(hit, values, 0.0), axis=-1, keepdims=True)
            held[0, pl.ds(row, size), :] = jnp.broadcast_to(lse, (size, 128))
            held[1, pl.ds(row, size), :] = jnp.broadcast_to(picked, (size, 128))
        on = diagonal()
        for j in range(rows // 128):
            for kind in range(2):
                tile = rows_at(held, kind, scalars_ref, 64 + 8 * j, 8)
                line = jnp.sum(jnp.where(on, tile, 0.0), axis=0, keepdims=True)
                out_ref[pl.ds(kind * (rows // 128) + j, 1), :] = line

    return pl.pallas_call(
        kernel,
        out_shape=jax.ShapeDtypeStruct((2 * rows // 128, 128), f32),
        in_specs=[SMEM] + [VMEM] * (2 * n),
        out_specs=VMEM,
        scratch_shapes=[pltpu.VMEM((2, rows, 128), f32)],
        compiler_params=pltpu.CompilerParams(vmem_limit_bytes=24 << 20),
    )(scalars, *logits, *facts)


def rows_at(held, kind, scalars_ref, number, count):
    found = []
    for k in range(count):
        place = pl.multiple_of(scalars_ref[number + k] * SLAB, SLAB)
        found.append(held[kind, pl.ds(place, SLAB), :])
    return jnp.concatenate(found)


def slopes_of(scalars, stats, logits, facts):
    n = len(logits)
    rows, columns = sum(v.shape[0] for v in logits), logits[0].shape[1]
    lines = rows // 128

    def kernel(scalars_ref, stats_ref, *refs):
        logit_refs, fact_refs = refs[:n], refs[n : 2 * n]
        out_ref, sums_ref, held = refs[2 * n :]
        each = [stats_ref[d, 0:lines, :] for d in range(stats.shape[0])]
        peak = functools.reduce(jnp.maximum, each)
        lse = peak + jnp.log(sum(jnp.exp(e - peak) for e in each))
        cross = lse - sum(stats_ref[d, lines : 2 * lines, :] for d in range(stats.shape[0]))
        on = diagonal()
        for kind, lined in enumerate((lse, cross)):
            for j in range(lines):
                tile = jnp.where(on, jnp.broadcast_to(lined[j : j + 1, :], (128, 128)), 0.0)
                column = jnp.sum(tile, axis=1, keepdims=True)
                held[kind, pl.ds(128 * j, 128), :] = jnp.broadcast_to(column, (128, 128))
        sums = [jnp.zeros((1, 128), f32) for _ in range(4)]
        for g, at, row, size in chunks(logits):
            fact = fact_refs[g][pl.ds(at, size), :].astype(f32)
            hit = hits(fact, columns, scalars_ref[128])
            weight, flag = fact[:, 2:3], fact[:, 3:4]
            blocks = (row // SLAB, size // SLAB)
            row_lse = rows_at(held, 0, scalars_ref, *blocks)[:, 0:1]
            row_cross = rows_at(held, 1, scalars_ref, *blocks)
            softmax = jnp.exp(logit_refs[g][pl.ds(at, size), :] - row_lse)
            scale = weight * jnp.where(flag > 0.0, step_decay, 1.0)
            slope = scale * (softmax - jnp.where(hit, 1.0, 0.0))
            out_ref[pl.ds(row, size), :] = slope.astype(bf16)
            for k, on_step in enumerate((weight * (1.0 - flag), weight * flag)):
                sums[k] += jnp.sum(on_step * row_cross, axis=0, keepdims=True)
                spread = jnp.broadcast_to(on_step, (size, 128))
                sums[2 + k] += jnp.sum(spread, axis=0, keepdims=True)
        for k in range(4):
            sums_ref[pl.ds(k, 1), :] = sums[k]
        sums_ref[pl.ds(4, 4), :] = jnp.zeros((4, 128), f32)

    return pl.pallas_call(
        kernel,
        out_shape=(
            jax.ShapeDtypeStruct((rows, columns), bf16),
            jax.ShapeDtypeStruct((8, 128), f32),
        ),
        in_specs=[SMEM] + [VMEM] * (1 + 2 * n),
        out_specs=(VMEM, VMEM),
        scratch_shapes=[pltpu.VMEM((2, rows, 128), f32)],
        compiler_params=pltpu.CompilerParams(vmem_limit_bytes=24 << 20),
    )(scalars, stats, *logits, *facts)


def gradient_blocks(pieces, slopes, features, depth, dtype):
    count, columns = features.shape[0], slopes.shape[1]
    n, counts = len(pieces), [c for _, c in pieces]
    rows = slopes.shape[0]

    def kernel(features_ref, *refs):
        slopes_ref, out_ref = refs[n:]
        for k in range(count):
            x = block_of(refs[:n], counts, features_ref[k] * depth, depth)
            found = lax.dot_general(
                x, slopes_ref[...], (((0,), (0,)), ((), ())), preferred_element_type=f32
            )
            out_ref[k] = found.astype(dtype)

    return pl.pallas_call(
        kernel,
        out_shape=jax.ShapeDtypeStruct((count, depth, columns), dtype),
        in_specs=[SMEM] + [VMEM] * (n + 1),
        out_specs=VMEM,
        compiler_params=pltpu.CompilerParams(vmem_limit_bytes=32 << 20),
        cost_estimate=pl.CostEstimate(
            flops=2 * rows * count * depth * columns,
            bytes_accessed=2 * count * depth * (rows + 2 * columns),
            transcendentals=0,
        ),
    )(features, *[p for p, _ in pieces], slopes)


def local(drafter_hidden, norm_gain, head_weight, labels, loss_mask, offsets):
    steps, local_tokens, width_part = drafter_hidden.shape
    vocab_part = head_weight.shape[1]
    width = width_part * 8
    core, half_x, row_y = lax.axis_index("c"), lax.axis_index("xh"), lax.axis_index("y")
    x_at, z_at = 2 * half_x + lax.axis_index("xl"), lax.axis_index("z")
    joined = lambda *pieces: jnp.concatenate(pieces)
    up = lambda v: along(v, "z", 1)
    down = lambda v: along(v, "z", -1)

    w0 = jnp.where(core == half_x, head_weight, crossed(head_weight))
    w1 = along(w0, "y", 1)

    with jax.named_scope("normed_rows"):
        facts = row_facts(labels, loss_mask, offsets, steps)
        parts = drafter_hidden.reshape(steps, 8, SLAB, width_part).swapaxes(0, 1)
        parts = parts.reshape(8, steps * SLAB, width_part)
        gains = jnp.broadcast_to(norm_gain, (8, 8, width_part))
        traded = lax.all_to_all(
            jnp.concatenate([parts, gains], axis=1), ("xh", "y"), split_axis=0, concat_axis=0, tiled=True
        )
        gain = traded[:, steps * SLAB].reshape(width)
        hidden = traded[:, : steps * SLAB].swapaxes(0, 1).reshape(steps * SLAB, width).astype(f32)
        inverse = lax.rsqrt(jnp.mean(hidden * hidden, axis=-1, keepdims=True) + epsilon)
        normed = (hidden * inverse * gain.astype(f32)).astype(bf16)
        rows = jnp.concatenate([normed, facts], axis=1)

    a, b = rows[:SLAB], rows[SLAB:]
    half = width_part // 2
    with jax.named_scope("round_1"):
        b1, b3, b2 = across_x(b, 1), across_x(b, 3), across_x(b, 2)
        u1, d1 = up(a), down(a)
    b1, b3, b2, u1, d1, w1 = together(b1, b3, b2, u1, d1, w1)
    with jax.named_scope("round_2"):
        own = joined(b, b1, b3, b2)
        zu2, zd2 = up(joined(own, u1)), down(joined(own, d1))
        near = joined(a, u1, d1)
        n1, n3 = across_x(near, 1), across_x(near, 3)
        w2 = along(w1, "y", 1)
    zu2, zd2, n1, n3, w2 = together(zu2, zd2, n1, n3, w2)
    with jax.named_scope("round_3"):
        zu3, zd3 = up(zu2), down(zd2)
        u2, d2 = zu2[64:], zd2[64:]
        xa, xb = across_x(joined(n3[:32], u2, d2), 1), across_x(joined(n1[32:], u2, d2), 3)
        w3 = along(w2, "y", 1)
    zu3, zd3, xa, xb, w3 = together(zu3, zd3, xa, xb, w3)
    with jax.named_scope("round_4"):
        zu4, zd4 = up(zu3), down(zd3)
        u3, d3 = zu3[64:], zd3[64:]
        xc, xd = across_x(joined(xb[16:32], u3, d3), 1), across_x(joined(xa[48:], u3, d3), 3)
        head_mine = jnp.stack([w0, w1, w2, w3])
        head_other = other_core(head_mine)
    zu4, zd4, xc, xd, head_other = together(zu4, zd4, xc, xd, head_other)
    with jax.named_scope("round_5"):
        v4, e4 = up(zu4[:32]), down(zd4[32:64])
        u4 = zu4[64:]
        xe, xf = across_x(joined(xd[16:32], u4), 1), across_x(joined(xc[32:], u4), 3)
        xg = across_x(u4, 2)

    first = lambda *listed: [(0, bits, z) for bits, zs in listed for z in zs]
    second = lambda z: [(1, bits, z) for bits in (0, 1, 3, 2)]
    early = [
        (a, first((0, (0,)))), (u1, first((0, (7,)))), (d1, first((0, (1,)))),
        (own, second(0)), (n1, first((1, (0, 7, 1)))), (n3, first((3, (0, 7, 1)))),
        (zu2, second(7) + first((0, (6,)))), (zd2, second(1) + first((0, (2,)))),
        (zu3, second(6) + first((0, (5,)))), (zd3, second(2) + first((0, (3,)))),
        (zu4, second(5) + first((0, (4,)))), (zd4, second(3)),
        (xa, first((2, (0, 7)), (1, (6, 2)))), (xb, first((2, (1,)), (3, (6, 2)))),
        (xc, first((2, (6,)), (1, (5, 3)))), (xd, first((2, (2,)), (3, (5, 3)))),
    ]
    late = [
        (v4, second(4)[:2]), (e4, second(4)[2:]),
        (xe, first((2, (5,)), (1, (4,)))), (xf, first((2, (3,)), (3, (4,)))), (xg, first((2, (4,)))),
    ]
    order = np.array([o for _, listed in early + late for o in listed], np.int32)
    early, late = ([(p, SLAB * len(o)) for p, o in group] for group in (early, late))
    slot = order[:, 0] * 32 + (order[:, 1] ^ x_at) * 8 + (order[:, 2] + z_at) % 8
    taken = jnp.sum(
        jnp.where(slot[None, :] == np.arange(64)[:, None], np.arange(64, dtype=np.int32), 0), axis=1
    )
    first_column = lax.axis_index(("xl", "z", "xh")) * vocab_part
    scalars = jnp.concatenate([slot, taken, first_column[None]]).astype(jnp.int32)
    at_y = (row_y - np.arange(4, dtype=np.int32)) % 4
    with jax.named_scope("logits"):
        by_head = jnp.concatenate([core * 4 + at_y, (1 - core) * 4 + at_y]).astype(jnp.int32)
        soon = logits_of(early, head_mine, head_other, by_head)
        *arrived, head_mine, head_other, soon_0, soon_1 = together(
            *[p for p, _ in late], head_mine, head_other, *soon
        )
        late = [(p, rows) for p, (_, rows) in zip(arrived, late)]
        then = logits_of(late, head_mine, head_other, by_head)
        pieces = early + late
        logits, facts = (soon_0, then[0]), (soon_1, then[1])
    with jax.named_scope("row_totals"):
        message = row_parts(scalars, logits, facts)
        stats = sent_to_all(message, ("xl", "z", "xh"))
    with jax.named_scope("slopes"):
        slopes, sums = slopes_of(scalars, stats, logits, facts)
    with jax.named_scope("gradient"):
        at = lambda owner, *by: (owner * 4 + (row_y + np.array(by, np.int32)) % 4).astype(jnp.int32)
        blocks = lambda index, dtype: gradient_blocks(pieces, slopes, index, width_part, dtype)
        far = blocks(at(1 - core, 2), bf16)
        far, slopes = together(far, slopes)
        far_taken, sums_taken = other_core(far), other_core(sums)
        far = blocks(at(core, 2), f32)
        far = (far + far_taken.astype(f32))[0].astype(bf16)
        far, sums_taken, slopes = together(far, sums_taken, slopes)
        relay_up, relay_down = along(far[:half], "y", 1), along(far[half:], "y", -1)
        sums = sums + sums_taken
        sums_y = [along(sums, "y", by) for by in (1, 3, 2)]
        near = blocks(at(1 - core, 1, 3), bf16)
        near, slopes = together(near, slopes)
        near_taken = other_core(near)
        near = blocks(at(core, 1, 3), f32)
        near = near + near_taken.astype(f32)
        ahead = joined(near[0, :half] + relay_up.astype(f32), near[0, half:]).astype(bf16)
        behind = joined(near[1, :half], near[1, half:] + relay_down.astype(f32)).astype(bf16)
        ahead, behind, slopes, *sums_y = together(ahead, behind, slopes, *sums_y)
        from_behind, from_ahead = along(ahead, "y", 1), along(behind, "y", -1)
        rest = blocks(at(1 - core, 0), bf16)
        rest, slopes = together(rest, slopes)
        rest_taken = other_core(rest)
        total = blocks(at(core, 0), f32)[0] + rest_taken[0].astype(f32)
        total = total + from_behind.astype(f32) + from_ahead.astype(f32)
        grad = jnp.where(core == half_x, total, crossed(total.astype(bf16)).astype(f32))
    with jax.named_scope("loss"):
        sums = sums + sum(sums_y)
        factors = step_decay ** jnp.arange(steps, dtype=f32)
        loss = jnp.sum(factors * sums[:steps, 0] / sums[steps : 2 * steps, 0])
    return loss, grad


def solution(mesh):
    inner = Mesh(mesh.devices.reshape(2, 8, 2, 2, 4), ("xl", "z", "c", "xh", "y"))
    dp, tensor = ("xl", "z", "c"), ("xh", "y")
    return jax.shard_map(
        local,
        mesh=inner,
        in_specs=(P(None, dp, tensor), P(tensor), P(tensor, dp), P(dp), P(dp), P()),
        out_specs=(P(), P(tensor, dp)),
        check_vma=False,
    )
```

```python
import functools

import jax
import jax.numpy as jnp
import numpy as np
from jax import lax
from jax.experimental import pallas as pl
from jax.experimental.pallas import tpu as pltpu
from jax.sharding import Mesh
from jax.sharding import PartitionSpec as P

WINDOW = 512
META = 128
SLAB = 16

epsilon = 1e-05
step_decay = 0.8

f32 = jnp.float32
bf16 = jnp.bfloat16


def across_x(value, bits):
    place = lambda p: (p % 2) * 2 + p // 2
    return lax.ppermute(value, ("xl", "xh"), [(place(p), place(p ^ bits)) for p in range(4)])


def along(value, axis, by):
    n = lax.axis_size(axis)
    return lax.ppermute(value, axis, [(i, (i + by) % n) for i in range(n)])


def other_core(value):
    return lax.ppermute(value, "c", [(0, 1), (1, 0)])


def crossed(value):
    return lax.ppermute(value, ("c", "xh"), [(1, 2), (2, 1)])


def sent_to_all(value, axis):
    copies = jnp.broadcast_to(value, (lax.axis_size(axis), *value.shape))
    return lax.all_to_all(copies, axis, split_axis=0, concat_axis=0, tiled=True)


def together(*values):
    return lax.optimization_barrier(values)


def row_facts(labels, loss_mask, offsets, steps):
    local_tokens = labels.shape[0]
    ways = lax.axis_size(("xl", "z", "c"))
    rank = lax.axis_index(("xl", "z", "c"))
    both = jnp.stack([labels, loss_mask])
    following = lax.ppermute(both, ("xl", "z", "c"), [(i, (i - 1) % ways) for i in range(ways)])
    following = jnp.where(rank == ways - 1, both[:, -1:], following)
    longer = jnp.concatenate([both, following], axis=1)
    at = lax.axis_index(("xh", "y")) * SLAB
    found = []
    for step in range(steps):
        piece = lax.dynamic_slice(longer, (0, at + offsets[step]), (2, SLAB))
        position = rank * local_tokens + at + jnp.arange(SLAB, dtype=jnp.int32)
        inside = position % WINDOW + offsets[step] < WINDOW
        weight = jnp.where(inside, piece[1], 0)
        flag = jnp.full_like(weight, step)
        found.append(jnp.stack([piece[0] // 128, piece[0] % 128, weight, flag], axis=-1))
    facts = jnp.stack(found).astype(bf16).reshape(steps * SLAB, 4)
    return jnp.pad(facts, ((0, 0), (0, META - facts.shape[-1])))


VMEM = pl.BlockSpec(memory_space=pltpu.VMEM)
SMEM = pl.BlockSpec(memory_space=pltpu.SMEM)


def block_of(refs, counts, at, width):
    columns = pl.ds(pl.multiple_of(at, width), width)
    return jnp.concatenate([r[pl.ds(0, count), columns] for r, count in zip(refs, counts)])


def logits_of(pieces, head_mine, head_other, features):
    n, counts = len(pieces), [count for _, count in pieces]
    arrays, rows = [p for p, _ in pieces], sum(counts)
    _, depth, columns = head_mine.shape
    meta_at = arrays[0].shape[1] - META

    def kernel(features_ref, *refs):
        head_mine_ref, head_other_ref, out_ref, facts_ref, rows_ref, held, sems = refs[n:]
        facts_ref[...] = block_of(refs[:n], counts, meta_at, META)
        copies = []
        for k in range(8):
            x = block_of(refs[:n], counts, features_ref[k] * depth, depth)
            if k >= 2:
                copies[k - 2].wait()
            held[k % 2] = x
            copies.append(pltpu.make_async_copy(held.at[k % 2], rows_ref.at[k], sems.at[k % 2]))
            copies[k].start()
            head = (head_mine_ref, head_other_ref)[k // 4][k % 4]
            found = jnp.dot(x, head, preferred_element_type=f32)
            if k == 0:
                out_ref[...] = found
            else:
                out_ref[...] += found
        copies[6].wait()
        copies[7].wait()

    return pl.pallas_call(
        kernel,
        out_shape=(
            jax.ShapeDtypeStruct((rows, columns), f32),
            jax.ShapeDtypeStruct((rows, META), bf16),
            jax.ShapeDtypeStruct((8, rows, depth), bf16),
        ),
        in_specs=[SMEM] + [VMEM] * (n + 2),
        out_specs=(VMEM, VMEM, pl.BlockSpec(memory_space=pl.ANY)),
        scratch_shapes=[pltpu.VMEM((2, rows, depth), bf16), pltpu.SemaphoreType.DMA((2,))],
        compiler_params=pltpu.CompilerParams(vmem_limit_bytes=16 << 20),
        cost_estimate=pl.CostEstimate(
            flops=2 * rows * 8 * depth * columns,
            bytes_accessed=2 * 8 * depth * (rows + columns),
            transcendentals=0,
        ),
    )(features, *arrays, head_mine, head_other)


def diagonal():
    return lax.broadcasted_iota(jnp.int32, (128, 128), 0) == lax.broadcasted_iota(
        jnp.int32, (128, 128), 1
    )


def hits(facts, columns, first):
    label = (facts[:, 0:1] * 128.0 + facts[:, 1:2]).astype(jnp.int32) - first
    return lax.broadcasted_iota(jnp.int32, (facts.shape[0], columns), 1) == label


def chunks(groups):
    start = 0
    for g, group in enumerate(groups):
        rows = group.shape[0]
        size = max(k for k in range(SLAB, 81, SLAB) if rows % k == 0)
        for at in range(0, rows, size):
            yield g, at, start + at, size
        start += rows


def row_parts(scalars, logits, facts):
    n = len(logits)
    rows, columns = sum(v.shape[0] for v in logits), logits[0].shape[1]

    def kernel(scalars_ref, *refs):
        logit_refs, fact_refs, (out_ref, held) = refs[:n], refs[n : 2 * n], refs[2 * n :]
        for g, at, row, size in chunks(logits):
            values = logit_refs[g][pl.ds(at, size), :]
            fact = fact_refs[g][pl.ds(at, size), :].astype(f32)
            hit = hits(fact, columns, scalars_ref[128])
            top = jnp.max(values, axis=-1, keepdims=True)
            lse = top + jnp.log(jnp.sum(jnp.exp(values - top), axis=-1, keepdims=True))
            picked = jnp.sum(jnp.where(hit, values, 0.0), axis=-1, keepdims=True)
            held[0, pl.ds(row, size), :] = jnp.broadcast_to(lse, (size, 128))
            held[1, pl.ds(row, size), :] = jnp.broadcast_to(picked, (size, 128))
        on = diagonal()
        for j in range(rows // 128):
            for kind in range(2):
                tile = rows_at(held, kind, scalars_ref, 64 + 8 * j, 8)
                line = jnp.sum(jnp.where(on, tile, 0.0), axis=0, keepdims=True)
                out_ref[pl.ds(kind * (rows // 128) + j, 1), :] = line

    return pl.pallas_call(
        kernel,
        out_shape=jax.ShapeDtypeStruct((2 * rows // 128, 128), f32),
        in_specs=[SMEM] + [VMEM] * (2 * n),
        out_specs=VMEM,
        scratch_shapes=[pltpu.VMEM((2, rows, 128), f32)],
        compiler_params=pltpu.CompilerParams(vmem_limit_bytes=8 << 20),
    )(scalars, *logits, *facts)


def rows_at(held, kind, scalars_ref, number, count):
    found = []
    for k in range(count):
        place = pl.multiple_of(scalars_ref[number + k] * SLAB, SLAB)
        found.append(held[kind, pl.ds(place, SLAB), :])
    return jnp.concatenate(found)


def slopes_of(scalars, stats, logits, facts):
    n = len(logits)
    rows, columns = sum(v.shape[0] for v in logits), logits[0].shape[1]
    lines = rows // 128

    def kernel(scalars_ref, stats_ref, *refs):
        given, (out_ref, sums_ref, held) = refs[: 2 * n], refs[2 * n : 2 * n + 3]
        brought, sems = refs[2 * n + 3 : -1], refs[-1]
        copies = [
            pltpu.make_async_copy(given[k], brought[k], sems.at[k]) for k in range(2 * n)
        ]
        for copy in copies:
            copy.start()
        logit_refs, fact_refs = brought[:n], brought[n:]
        each = [stats_ref[d, 0:lines, :] for d in range(stats.shape[0])]
        peak = functools.reduce(jnp.maximum, each)
        lse = peak + jnp.log(sum(jnp.exp(e - peak) for e in each))
        cross = lse - sum(stats_ref[d, lines : 2 * lines, :] for d in range(stats.shape[0]))
        on = diagonal()
        for kind, lined in enumerate((lse, cross)):
            for j in range(lines):
                tile = jnp.where(on, jnp.broadcast_to(lined[j : j + 1, :], (128, 128)), 0.0)
                column = jnp.sum(tile, axis=1, keepdims=True)
                held[kind, pl.ds(128 * j, 128), :] = jnp.broadcast_to(column, (128, 128))
        for copy in copies:
            copy.wait()
        sums = [jnp.zeros((1, 128), f32) for _ in range(4)]
        for g, at, row, size in chunks(logits):
            fact = fact_refs[g][pl.ds(at, size), :].astype(f32)
            hit = hits(fact, columns, scalars_ref[128])
            weight, flag = fact[:, 2:3], fact[:, 3:4]
            blocks = (row // SLAB, size // SLAB)
            row_lse = rows_at(held, 0, scalars_ref, *blocks)[:, 0:1]
            row_cross = rows_at(held, 1, scalars_ref, *blocks)
            softmax = jnp.exp(logit_refs[g][pl.ds(at, size), :] - row_lse)
            scale = weight * jnp.where(flag > 0.0, step_decay, 1.0)
            slope = scale * (softmax - jnp.where(hit, 1.0, 0.0))
            out_ref[pl.ds(row, size), :] = slope.astype(bf16)
            for k, on_step in enumerate((weight * (1.0 - flag), weight * flag)):
                sums[k] += jnp.sum(on_step * row_cross, axis=0, keepdims=True)
                spread = jnp.broadcast_to(on_step, (size, 128))
                sums[2 + k] += jnp.sum(spread, axis=0, keepdims=True)
        for k in range(4):
            sums_ref[pl.ds(k, 1), :] = sums[k]
        sums_ref[pl.ds(4, 4), :] = jnp.zeros((4, 128), f32)

    return pl.pallas_call(
        kernel,
        out_shape=(
            jax.ShapeDtypeStruct((rows, columns), bf16),
            jax.ShapeDtypeStruct((8, 128), f32),
        ),
        in_specs=[SMEM, VMEM] + [pl.BlockSpec(memory_space=pl.ANY)] * (2 * n),
        out_specs=(VMEM, VMEM),
        scratch_shapes=[
            pltpu.VMEM((2, rows, 128), f32),
            *[pltpu.VMEM(v.shape, v.dtype) for v in (*logits, *facts)],
            pltpu.SemaphoreType.DMA((2 * n,)),
        ],
        compiler_params=pltpu.CompilerParams(vmem_limit_bytes=8 << 20),
    )(scalars, stats, *logits, *facts)


def gradient_blocks(blocks, slopes, start, step, count, dtype):
    _, _, depth = blocks[0].shape
    rows, columns = slopes.shape

    def kernel(*refs):
        slopes_ref, out_ref = refs[-2:]
        x = jnp.concatenate([r[0] for r in refs[:-2]])
        found = lax.dot_general(
            x, slopes_ref[...], (((0,), (0,)), ((), ())), preferred_element_type=f32
        )
        out_ref[0] = found.astype(dtype)

    return pl.pallas_call(
        kernel,
        out_shape=jax.ShapeDtypeStruct((count, depth, columns), dtype),
        grid=(count,),
        in_specs=[
            *[pl.BlockSpec((1, b.shape[1], depth), lambda k: (start + step * k, 0, 0)) for b in blocks],
            VMEM,
        ],
        out_specs=pl.BlockSpec((1, depth, columns), lambda k: (k, 0, 0)),
        compiler_params=pltpu.CompilerParams(vmem_limit_bytes=16 << 20),
        cost_estimate=pl.CostEstimate(
            flops=2 * rows * count * depth * columns,
            bytes_accessed=2 * count * depth * (rows + 2 * columns),
            transcendentals=0,
        ),
    )(*blocks, slopes)


def local(drafter_hidden, norm_gain, head_weight, labels, loss_mask, offsets):
    steps, local_tokens, width_part = drafter_hidden.shape
    vocab_part = head_weight.shape[1]
    width = width_part * 8
    core, half_x, row_y = lax.axis_index("c"), lax.axis_index("xh"), lax.axis_index("y")
    x_at, z_at = 2 * half_x + lax.axis_index("xl"), lax.axis_index("z")
    joined = lambda *pieces: jnp.concatenate(pieces)
    up = lambda v: along(v, "z", 1)
    down = lambda v: along(v, "z", -1)

    swapped = crossed(head_weight)

    with jax.named_scope("normed_rows"):
        facts = row_facts(labels, loss_mask, offsets, steps)
        parts = drafter_hidden.reshape(steps, 8, SLAB, width_part).swapaxes(0, 1)
        parts = parts.reshape(8, steps * SLAB, width_part)
        gains = jnp.broadcast_to(norm_gain, (8, 8, width_part))
        traded = lax.all_to_all(
            jnp.concatenate([parts, gains], axis=1), ("xh", "y"), split_axis=0, concat_axis=0, tiled=True
        )
        gain = traded[:, steps * SLAB].reshape(width)
        hidden = traded[:, : steps * SLAB].swapaxes(0, 1).reshape(steps * SLAB, width).astype(f32)
        inverse = lax.rsqrt(jnp.mean(hidden * hidden, axis=-1, keepdims=True) + epsilon)
        normed = (hidden * inverse * gain.astype(f32)).astype(bf16)
        rows = jnp.concatenate([normed, facts], axis=1)

    a, b = rows[:SLAB], rows[SLAB:]
    half = width_part // 2
    with jax.named_scope("round_1"):
        b1, b3, b2 = across_x(b, 1), across_x(b, 3), across_x(b, 2)
        u1, d1 = up(a), down(a)
    b1, b3, b2, u1, d1, swapped = together(b1, b3, b2, u1, d1, swapped)
    with jax.named_scope("round_2"):
        own = joined(b, b1, b3, b2)
        zu2, zd2 = up(joined(own, u1)), down(joined(own, d1))
        near = joined(a, u1, d1)
        n1, n3 = across_x(near, 1), across_x(near, 3)
        w0 = jnp.where(core == half_x, head_weight, swapped)
        w1, w3 = along(w0, "y", 1), along(w0, "y", -1)
    zu2, zd2, n1, n3, w1, w3 = together(zu2, zd2, n1, n3, w1, w3)
    with jax.named_scope("round_3"):
        zu3, zd3 = up(zu2), down(zd2)
        u2, d2 = zu2[64:], zd2[64:]
        xa, xb = across_x(joined(n3[:32], u2, d2), 1), across_x(joined(n1[32:], u2, d2), 3)
        w2 = along(w1, "y", 1)
    zu3, zd3, xa, xb, w2 = together(zu3, zd3, xa, xb, w2)
    with jax.named_scope("round_4"):
        zu4, zd4 = up(zu3), down(zd3)
        u3, d3 = zu3[64:], zd3[64:]
        xc, xd = across_x(joined(xb[16:32], u3, d3), 1), across_x(joined(xa[48:], u3, d3), 3)
        head_mine = jnp.stack([w0, w1, w2, w3])
        head_other = other_core(head_mine)
    zu4, zd4, xc, xd, head_other = together(zu4, zd4, xc, xd, head_other)
    with jax.named_scope("round_5"):
        v4, e4 = up(zu4[:32]), down(zd4[32:64])
        u4 = zu4[64:]
        xe, xf = across_x(joined(xd[16:32], u4), 1), across_x(joined(xc[32:], u4), 3)
        xg = across_x(u4, 2)

    first = lambda *listed: [(0, bits, z) for bits, zs in listed for z in zs]
    second = lambda z: [(1, bits, z) for bits in (0, 1, 3, 2)]
    early = [
        (a, first((0, (0,)))), (u1, first((0, (7,)))), (d1, first((0, (1,)))),
        (own, second(0)), (n1, first((1, (0, 7, 1)))), (n3, first((3, (0, 7, 1)))),
        (zu2, second(7) + first((0, (6,)))), (zd2, second(1) + first((0, (2,)))),
        (zu3, second(6) + first((0, (5,)))), (zd3, second(2) + first((0, (3,)))),
        (zu4, second(5) + first((0, (4,)))), (zd4, second(3)),
        (xa, first((2, (0, 7)), (1, (6, 2)))), (xb, first((2, (1,)), (3, (6, 2)))),
        (xc, first((2, (6,)), (1, (5, 3)))), (xd, first((2, (2,)), (3, (5, 3)))),
    ]
    late = [
        (v4, second(4)[:2]), (e4, second(4)[2:]),
        (xe, first((2, (5,)), (1, (4,)))), (xf, first((2, (3,)), (3, (4,)))), (xg, first((2, (4,)))),
    ]
    order = np.array([o for _, listed in early + late for o in listed], np.int32)
    early, late = ([(p, SLAB * len(o)) for p, o in group] for group in (early, late))
    slot = order[:, 0] * 32 + (order[:, 1] ^ x_at) * 8 + (order[:, 2] + z_at) % 8
    taken = jnp.sum(
        jnp.where(slot[None, :] == np.arange(64)[:, None], np.arange(64, dtype=np.int32), 0), axis=1
    )
    first_column = lax.axis_index(("xl", "z", "xh")) * vocab_part
    scalars = jnp.concatenate([slot, taken, first_column[None]]).astype(jnp.int32)
    at_y = (row_y - np.arange(4, dtype=np.int32)) % 4
    with jax.named_scope("logits"):
        by_head = jnp.concatenate([core * 4 + at_y, (1 - core) * 4 + at_y]).astype(jnp.int32)
        soon = logits_of(early, head_mine, head_other, by_head)
        *arrived, head_mine, head_other, soon_0, soon_1, soon_2 = together(
            *[p for p, _ in late], head_mine, head_other, *soon
        )
        late = [(p, rows) for p, (_, rows) in zip(arrived, late)]
        then = logits_of(late, head_mine, head_other, by_head)
        logits, facts, wide = (soon_0, then[0]), (soon_1, then[1]), (soon_2, then[2])
    with jax.named_scope("row_totals"):
        message = row_parts(scalars, logits, facts)
        stats = sent_to_all(message, ("xl", "z", "xh"))
    with jax.named_scope("slopes"):
        slopes, sums = slopes_of(scalars, stats, logits, facts)
    with jax.named_scope("gradient"):
        blocks = lambda *at: gradient_blocks(wide, slopes, *at)
        far = blocks(6, 0, 1, bf16)
        far, slopes = together(far, slopes)
        far_taken, sums_taken = other_core(far), other_core(sums)
        far = blocks(2, 0, 1, f32)
        far = (far + far_taken.astype(f32))[0].astype(bf16)
        far, sums, slopes = together(far, sums + sums_taken, slopes)
        relay_up, relay_down = along(far[:half], "y", 1), along(far[half:], "y", -1)
        near = blocks(7, -2, 2, bf16)
        near, slopes = together(near, slopes)
        near_taken = other_core(near)
        near = blocks(3, -2, 2, f32)
        sums, near_taken, relay_up, relay_down = together(sums, near_taken, relay_up, relay_down)
        sums = sums + along(sums, "y", 2)
        near = near + near_taken.astype(f32)
        ahead = joined(near[0, :half] + relay_up.astype(f32), near[0, half:]).astype(bf16)
        behind = joined(near[1, :half], near[1, half:] + relay_down.astype(f32)).astype(bf16)
        ahead, behind, slopes = together(ahead, behind, slopes)
        from_behind, from_ahead = along(ahead, "y", 1), along(behind, "y", -1)
        rest = blocks(4, 0, 1, bf16)
        rest, slopes = together(rest, slopes)
        rest_taken = other_core(rest)
        total = blocks(0, 0, 1, f32)[0] + rest_taken[0].astype(f32)
        total = total + from_behind.astype(f32) + from_ahead.astype(f32)
        grad = jnp.where(core == half_x, total, crossed(total.astype(bf16)).astype(f32))
    with jax.named_scope("loss"):
        sums = sums + along(sums, "y", 1)
        factors = step_decay ** jnp.arange(steps, dtype=f32)
        loss = jnp.sum(factors * sums[:steps, 0] / sums[steps : 2 * steps, 0])
    return loss, grad


def solution(mesh):
    inner = Mesh(mesh.devices.reshape(2, 8, 2, 2, 4), ("xl", "z", "c", "xh", "y"))
    dp, tensor = ("xl", "z", "c"), ("xh", "y")
    return jax.shard_map(
        local,
        mesh=inner,
        in_specs=(P(None, dp, tensor), P(tensor), P(tensor, dp), P(dp), P(dp), P()),
        out_specs=(P(), P(tensor, dp)),
        check_vma=False,
    )
```

```python
import functools

import jax
import jax.numpy as jnp
import numpy as np
from jax import lax
from jax.experimental import pallas as pl
from jax.experimental.pallas import tpu as pltpu
from jax.sharding import Mesh
from jax.sharding import PartitionSpec as P

WINDOW = 512
META = 128
SLAB = 16

epsilon = 1e-05
step_decay = 0.8

f32 = jnp.float32
bf16 = jnp.bfloat16


def across_x(value, bits):
    place = lambda p: (p % 2) * 2 + p // 2
    return lax.ppermute(value, ("xl", "xh"), [(place(p), place(p ^ bits)) for p in range(4)])


def along(value, axis, by):
    n = lax.axis_size(axis)
    return lax.ppermute(value, axis, [(i, (i + by) % n) for i in range(n)])


def other_core(value):
    return lax.ppermute(value, "c", [(0, 1), (1, 0)])


def crossed(value):
    return lax.ppermute(value, ("c", "xh"), [(1, 2), (2, 1)])


def sent_to_all(value, axis):
    copies = jnp.broadcast_to(value, (lax.axis_size(axis), *value.shape))
    return lax.all_to_all(copies, axis, split_axis=0, concat_axis=0, tiled=True)


def together(*values):
    return lax.optimization_barrier(values)


def row_facts(labels, loss_mask, offsets, steps):
    local_tokens = labels.shape[0]
    ways = lax.axis_size(("xl", "z", "c"))
    rank = lax.axis_index(("xl", "z", "c"))
    both = jnp.stack([labels, loss_mask])
    following = lax.ppermute(both, ("xl", "z", "c"), [(i, (i - 1) % ways) for i in range(ways)])
    following = jnp.where(rank == ways - 1, both[:, -1:], following)
    longer = jnp.concatenate([both, following], axis=1)
    at = lax.axis_index(("xh", "y")) * SLAB
    found = []
    for step in range(steps):
        piece = lax.dynamic_slice(longer, (0, at + offsets[step]), (2, SLAB))
        position = rank * local_tokens + at + jnp.arange(SLAB, dtype=jnp.int32)
        inside = position % WINDOW + offsets[step] < WINDOW
        weight = jnp.where(inside, piece[1], 0)
        flag = jnp.full_like(weight, step)
        found.append(jnp.stack([piece[0] // 128, piece[0] % 128, weight, flag], axis=-1))
    facts = jnp.stack(found).astype(bf16).reshape(steps * SLAB, 4)
    return jnp.pad(facts, ((0, 0), (0, META - facts.shape[-1])))


VMEM = pl.BlockSpec(memory_space=pltpu.VMEM)
SMEM = pl.BlockSpec(memory_space=pltpu.SMEM)


def block_of(refs, counts, at, width):
    columns = pl.ds(pl.multiple_of(at, width), width)
    return jnp.concatenate([r[pl.ds(0, count), columns] for r, count in zip(refs, counts)])


def logits_of(pieces, head_mine, head_other, features):
    n, counts = len(pieces), [count for _, count in pieces]
    arrays, rows = [p for p, _ in pieces], sum(counts)
    _, depth, columns = head_mine.shape
    meta_at = arrays[0].shape[1] - META

    def kernel(features_ref, *refs):
        head_mine_ref, head_other_ref, out_ref, facts_ref, rows_ref, held, sems = refs[n:]
        facts_ref[...] = block_of(refs[:n], counts, meta_at, META)
        copies = []
        for k in range(8):
            x = block_of(refs[:n], counts, features_ref[k] * depth, depth)
            if k >= 2:
                copies[k - 2].wait()
            held[k % 2] = x
            copies.append(pltpu.make_async_copy(held.at[k % 2], rows_ref.at[k], sems.at[k % 2]))
            copies[k].start()
            head = (head_mine_ref, head_other_ref)[k // 4][k % 4]
            found = jnp.dot(x, head, preferred_element_type=f32)
            if k == 0:
                out_ref[...] = found
            else:
                out_ref[...] += found
        copies[6].wait()
        copies[7].wait()

    return pl.pallas_call(
        kernel,
        out_shape=(
            jax.ShapeDtypeStruct((rows, columns), f32),
            jax.ShapeDtypeStruct((rows, META), bf16),
            jax.ShapeDtypeStruct((8, rows, depth), bf16),
        ),
        in_specs=[SMEM] + [VMEM] * (n + 2),
        out_specs=(VMEM, VMEM, pl.BlockSpec(memory_space=pl.ANY)),
        scratch_shapes=[pltpu.VMEM((2, rows, depth), bf16), pltpu.SemaphoreType.DMA((2,))],
        compiler_params=pltpu.CompilerParams(vmem_limit_bytes=16 << 20),
        cost_estimate=pl.CostEstimate(
            flops=2 * rows * 8 * depth * columns,
            bytes_accessed=2 * 8 * depth * (rows + columns),
            transcendentals=0,
        ),
    )(features, *arrays, head_mine, head_other)


def diagonal():
    return lax.broadcasted_iota(jnp.int32, (128, 128), 0) == lax.broadcasted_iota(
        jnp.int32, (128, 128), 1
    )


def hits(facts, columns, first):
    label = (facts[:, 0:1] * 128.0 + facts[:, 1:2]).astype(jnp.int32) - first
    return lax.broadcasted_iota(jnp.int32, (facts.shape[0], columns), 1) == label


def chunks(groups):
    start = 0
    for g, group in enumerate(groups):
        rows = group.shape[0]
        size = max(k for k in range(SLAB, 81, SLAB) if rows % k == 0)
        for at in range(0, rows, size):
            yield g, at, start + at, size
        start += rows


def row_parts(scalars, logits, facts):
    n = len(logits)
    rows, columns = sum(v.shape[0] for v in logits), logits[0].shape[1]

    def kernel(scalars_ref, *refs):
        logit_refs, fact_refs, (out_ref, held) = refs[:n], refs[n : 2 * n], refs[2 * n :]
        for g, at, row, size in chunks(logits):
            values = logit_refs[g][pl.ds(at, size), :]
            fact = fact_refs[g][pl.ds(at, size), :].astype(f32)
            hit = hits(fact, columns, scalars_ref[128])
            top = jnp.max(values, axis=-1, keepdims=True)
            lse = top + jnp.log(jnp.sum(jnp.exp(values - top), axis=-1, keepdims=True))
            picked = jnp.sum(jnp.where(hit, values, 0.0), axis=-1, keepdims=True)
            held[0, pl.ds(row, size), :] = jnp.broadcast_to(lse, (size, 128))
            held[1, pl.ds(row, size), :] = jnp.broadcast_to(picked, (size, 128))
        on = diagonal()
        for j in range(rows // 128):
            for kind in range(2):
                tile = rows_at(held, kind, scalars_ref, 64 + 8 * j, 8)
                line = jnp.sum(jnp.where(on, tile, 0.0), axis=0, keepdims=True)
                out_ref[pl.ds(kind * (rows // 128) + j, 1), :] = line

    return pl.pallas_call(
        kernel,
        out_shape=jax.ShapeDtypeStruct((2 * rows // 128, 128), f32),
        in_specs=[SMEM] + [VMEM] * (2 * n),
        out_specs=VMEM,
        scratch_shapes=[pltpu.VMEM((2, rows, 128), f32)],
        compiler_params=pltpu.CompilerParams(vmem_limit_bytes=8 << 20),
    )(scalars, *logits, *facts)


def rows_at(held, kind, scalars_ref, number, count):
    found = []
    for k in range(count):
        place = pl.multiple_of(scalars_ref[number + k] * SLAB, SLAB)
        found.append(held[kind, pl.ds(place, SLAB), :])
    return jnp.concatenate(found)


def slopes_of(scalars, stats, logits, facts):
    n = len(logits)
    rows, columns = sum(v.shape[0] for v in logits), logits[0].shape[1]
    lines = rows // 128

    def kernel(scalars_ref, stats_ref, *refs):
        given, (out_ref, sums_ref, held) = refs[: 2 * n], refs[2 * n : 2 * n + 3]
        brought, sems = refs[2 * n + 3 : -1], refs[-1]
        copies = [
            pltpu.make_async_copy(given[k], brought[k], sems.at[k]) for k in range(2 * n)
        ]
        for copy in copies:
            copy.start()
        logit_refs, fact_refs = brought[:n], brought[n:]
        each = [stats_ref[d, 0:lines, :] for d in range(stats.shape[0])]
        peak = functools.reduce(jnp.maximum, each)
        lse = peak + jnp.log(sum(jnp.exp(e - peak) for e in each))
        cross = lse - sum(stats_ref[d, lines : 2 * lines, :] for d in range(stats.shape[0]))
        on = diagonal()
        for kind, lined in enumerate((lse, cross)):
            for j in range(lines):
                tile = jnp.where(on, jnp.broadcast_to(lined[j : j + 1, :], (128, 128)), 0.0)
                column = jnp.sum(tile, axis=1, keepdims=True)
                held[kind, pl.ds(128 * j, 128), :] = jnp.broadcast_to(column, (128, 128))
        for copy in copies:
            copy.wait()
        sums = [jnp.zeros((1, 128), f32) for _ in range(4)]
        for g, at, row, size in chunks(logits):
            fact = fact_refs[g][pl.ds(at, size), :].astype(f32)
            hit = hits(fact, columns, scalars_ref[128])
            weight, flag = fact[:, 2:3], fact[:, 3:4]
            blocks = (row // SLAB, size // SLAB)
            row_lse = rows_at(held, 0, scalars_ref, *blocks)[:, 0:1]
            row_cross = rows_at(held, 1, scalars_ref, *blocks)
            softmax = jnp.exp(logit_refs[g][pl.ds(at, size), :] - row_lse)
            scale = weight * jnp.where(flag > 0.0, step_decay, 1.0)
            slope = scale * (softmax - jnp.where(hit, 1.0, 0.0))
            out_ref[pl.ds(row, size), :] = slope.astype(bf16)
            for k, on_step in enumerate((weight * (1.0 - flag), weight * flag)):
                sums[k] += jnp.sum(on_step * row_cross, axis=0, keepdims=True)
                spread = jnp.broadcast_to(on_step, (size, 128))
                sums[2 + k] += jnp.sum(spread, axis=0, keepdims=True)
        for k in range(4):
            sums_ref[pl.ds(k, 1), :] = sums[k]
        sums_ref[pl.ds(4, 4), :] = jnp.zeros((4, 128), f32)

    return pl.pallas_call(
        kernel,
        out_shape=(
            jax.ShapeDtypeStruct((rows, columns), bf16),
            jax.ShapeDtypeStruct((8, 128), f32),
        ),
        in_specs=[SMEM, VMEM] + [pl.BlockSpec(memory_space=pl.ANY)] * (2 * n),
        out_specs=(VMEM, VMEM),
        scratch_shapes=[
            pltpu.VMEM((2, rows, 128), f32),
            *[pltpu.VMEM(v.shape, v.dtype) for v in (*logits, *facts)],
            pltpu.SemaphoreType.DMA((2 * n,)),
        ],
        compiler_params=pltpu.CompilerParams(vmem_limit_bytes=8 << 20),
    )(scalars, stats, *logits, *facts)


def gradient_blocks(blocks, slopes, start, step, count, dtype):
    _, _, depth = blocks[0].shape
    rows, columns = slopes.shape

    def kernel(*refs):
        slopes_ref, out_ref = refs[-2:]
        x = jnp.concatenate([r[0] for r in refs[:-2]])
        found = lax.dot_general(
            x, slopes_ref[...], (((0,), (0,)), ((), ())), preferred_element_type=f32
        )
        out_ref[0] = found.astype(dtype)

    return pl.pallas_call(
        kernel,
        out_shape=jax.ShapeDtypeStruct((count, depth, columns), dtype),
        grid=(count,),
        in_specs=[
            *[pl.BlockSpec((1, b.shape[1], depth), lambda k: (start + step * k, 0, 0)) for b in blocks],
            VMEM,
        ],
        out_specs=pl.BlockSpec((1, depth, columns), lambda k: (k, 0, 0)),
        compiler_params=pltpu.CompilerParams(vmem_limit_bytes=16 << 20),
        cost_estimate=pl.CostEstimate(
            flops=2 * rows * count * depth * columns,
            bytes_accessed=2 * count * depth * (rows + 2 * columns),
            transcendentals=0,
        ),
    )(*blocks, slopes)


def local(drafter_hidden, norm_gain, head_weight, labels, loss_mask, offsets):
    steps, local_tokens, width_part = drafter_hidden.shape
    vocab_part = head_weight.shape[1]
    width = width_part * 8
    core, half_x, row_y = lax.axis_index("c"), lax.axis_index("xh"), lax.axis_index("y")
    x_at, z_at = 2 * half_x + lax.axis_index("xl"), lax.axis_index("z")
    joined = lambda *pieces: jnp.concatenate(pieces)
    up = lambda v: along(v, "z", 1)
    down = lambda v: along(v, "z", -1)

    swapped = crossed(head_weight)

    with jax.named_scope("normed_rows"):
        facts = row_facts(labels, loss_mask, offsets, steps)
        parts = [step.reshape(8, SLAB, width_part) for step in drafter_hidden]
        gains = jnp.broadcast_to(norm_gain, (8, 8, width_part))
        traded = lax.all_to_all(
            jnp.concatenate([*parts, gains], axis=1), ("xh", "y"), split_axis=0, concat_axis=0, tiled=True
        )
        gain = traded[:, steps * SLAB].reshape(width)
        hidden = traded[:, : steps * SLAB].swapaxes(0, 1).reshape(steps * SLAB, width).astype(f32)
        inverse = lax.rsqrt(jnp.mean(hidden * hidden, axis=-1, keepdims=True) + epsilon)
        normed = (hidden * inverse * gain.astype(f32)).astype(bf16)
        rows = jnp.concatenate([normed, facts], axis=1)

    a, b = rows[:SLAB], rows[SLAB:]
    with jax.named_scope("round_1"):
        b1, b3, b2 = across_x(b, 1), across_x(b, 3), across_x(b, 2)
        u1, d1 = up(a), down(a)
    b1, b3, b2, u1, d1, swapped = together(b1, b3, b2, u1, d1, swapped)
    with jax.named_scope("round_2"):
        own = joined(b, b1, b3, b2)
        zu2, zd2 = up(joined(own, u1)), down(joined(own, d1))
        near = joined(a, u1, d1)
        n1, n3 = across_x(near, 1), across_x(near, 3)
        w0 = jnp.where(core == half_x, head_weight, swapped)
        w1, w3 = along(w0, "y", 1), along(w0, "y", -1)
    zu2, zd2, n1, n3, w1, w3 = together(zu2, zd2, n1, n3, w1, w3)
    with jax.named_scope("round_3"):
        zu3, zd3 = up(zu2), down(zd2)
        u2, d2 = zu2[64:], zd2[64:]
        xa, xb = across_x(joined(n3[:32], u2, d2), 1), across_x(joined(n1[32:], u2, d2), 3)
        w2 = along(w1, "y", 1)
    zu3, zd3, xa, xb, w2 = together(zu3, zd3, xa, xb, w2)
    with jax.named_scope("round_4"):
        zu4, zd4 = up(zu3), down(zd3)
        u3, d3 = zu3[64:], zd3[64:]
        xc, xd = across_x(joined(xb[16:32], u3, d3), 1), across_x(joined(xa[48:], u3, d3), 3)
        head_mine = jnp.stack([w0, w1, w2, w3])
        head_other = other_core(head_mine)
    zu4, zd4, xc, xd, head_other = together(zu4, zd4, xc, xd, head_other)
    with jax.named_scope("round_5"):
        v4, e4 = up(zu4[:32]), down(zd4[32:64])
        u4 = zu4[64:]
        xe, xf = across_x(joined(xd[16:32], u4), 1), across_x(joined(xc[32:], u4), 3)
        xg = across_x(u4, 2)

    first = lambda *listed: [(0, bits, z) for bits, zs in listed for z in zs]
    second = lambda z: [(1, bits, z) for bits in (0, 1, 3, 2)]
    early = [
        (a, first((0, (0,)))), (u1, first((0, (7,)))), (d1, first((0, (1,)))),
        (own, second(0)), (n1, first((1, (0, 7, 1)))), (n3, first((3, (0, 7, 1)))),
        (zu2, second(7) + first((0, (6,)))), (zd2, second(1) + first((0, (2,)))),
        (zu3, second(6) + first((0, (5,)))), (zd3, second(2) + first((0, (3,)))),
        (zu4, second(5) + first((0, (4,)))), (zd4, second(3)),
        (xa, first((2, (0, 7)), (1, (6, 2)))), (xb, first((2, (1,)), (3, (6, 2)))),
        (xc, first((2, (6,)), (1, (5, 3)))), (xd, first((2, (2,)), (3, (5, 3)))),
    ]
    late = [
        (v4, second(4)[:2]), (e4, second(4)[2:]),
        (xe, first((2, (5,)), (1, (4,)))), (xf, first((2, (3,)), (3, (4,)))), (xg, first((2, (4,)))),
    ]
    order = np.array([o for _, listed in early + late for o in listed], np.int32)
    early, late = ([(p, SLAB * len(o)) for p, o in group] for group in (early, late))
    slot = order[:, 0] * 32 + (order[:, 1] ^ x_at) * 8 + (order[:, 2] + z_at) % 8
    taken = jnp.sum(
        jnp.where(slot[None, :] == np.arange(64)[:, None], np.arange(64, dtype=np.int32), 0), axis=1
    )
    first_column = lax.axis_index(("xl", "z", "xh")) * vocab_part
    scalars = jnp.concatenate([slot, taken, first_column[None]]).astype(jnp.int32)
    at_y = (row_y - np.arange(4, dtype=np.int32)) % 4
    with jax.named_scope("logits"):
        by_head = jnp.concatenate([core * 4 + at_y, (1 - core) * 4 + at_y]).astype(jnp.int32)
        soon = logits_of(early, head_mine, head_other, by_head)
        *arrived, head_mine, head_other, soon_0, soon_1, soon_2 = together(
            *[p for p, _ in late], head_mine, head_other, *soon
        )
        late = [(p, rows) for p, (_, rows) in zip(arrived, late)]
        then = logits_of(late, head_mine, head_other, by_head)
        logits, facts, wide = (soon_0, then[0]), (soon_1, then[1]), (soon_2, then[2])
    with jax.named_scope("row_totals"):
        message = row_parts(scalars, logits, facts)
        stats = sent_to_all(message, ("xl", "z", "xh"))
    with jax.named_scope("slopes"):
        slopes, sums = slopes_of(scalars, stats, logits, facts)
    with jax.named_scope("gradient"):
        blocks = lambda *at: gradient_blocks(wide, slopes, *at)
        far = blocks(6, 0, 1, bf16)
        far, slopes = together(far, slopes)
        far_taken, sums_taken = other_core(far), other_core(sums)
        far = blocks(2, 0, 1, f32)
        far = (far + far_taken.astype(f32))[0].astype(bf16)
        far, sums, slopes = together(far, sums + sums_taken, slopes)
        from_far = along(far, "y", 2)
        near = blocks(7, -2, 2, bf16)
        near, slopes = together(near, slopes)
        near_taken = other_core(near)
        near = blocks(3, -2, 2, f32)
        near = (near + near_taken.astype(f32)).astype(bf16)
        near, sums, slopes = together(near, sums, slopes)
        sums = sums + along(sums, "y", 2)
        ahead, behind = near[0], near[1]
        from_behind, from_ahead = along(ahead, "y", 1), along(behind, "y", -1)
        rest = blocks(4, 0, 1, bf16)
        rest, slopes = together(rest, slopes)
        rest_taken = other_core(rest)
        total = blocks(0, 0, 1, f32)[0] + rest_taken[0].astype(f32)
        total = total + from_behind.astype(f32) + from_ahead.astype(f32) + from_far.astype(f32)
        grad = jnp.where(core == half_x, total, crossed(total.astype(bf16)).astype(f32))
    with jax.named_scope("loss"):
        sums = sums + along(sums, "y", 1)
        factors = step_decay ** jnp.arange(steps, dtype=f32)
        loss = jnp.sum(factors * sums[:steps, 0] / sums[steps : 2 * steps, 0])
    return loss, grad


def solution(mesh):
    inner = Mesh(mesh.devices.reshape(2, 8, 2, 2, 4), ("xl", "z", "c", "xh", "y"))
    dp, tensor = ("xl", "z", "c"), ("xh", "y")
    return jax.shard_map(
        local,
        mesh=inner,
        in_specs=(P(None, dp, tensor), P(tensor), P(tensor, dp), P(dp), P(dp), P()),
        out_specs=(P(), P(tensor, dp)),
        check_vma=False,
    )
```
